1024 devices in a mesh: pipe: 8 (over y), dp: 32 (over z, core), tensor: 4 (over x).
Axes of the slice: x: 4, y: 8, z: 16, core: 2. Of those that a mesh axis runs over, the one named last changes fastest.
Arguments:
- activations: bfloat16 [8, 2, 4096, 16384], P('pipe', None, 'dp', 'tensor'), may hold values from -6 to 6
- cotangent: bfloat16 [8, 2, 4096, 1024], P('pipe', None, 'dp', 'tensor'), may hold values from -0.5 to 0.5
- error_tiles: bfloat16 [8, 32, 4, 4, 4, 128, 128], P('pipe', 'dp', 'tensor'), may hold values from -4 to 4
- tile_picks: int32 [8, 32, 4, 4, 4, 2], P('pipe', None, 'tensor'), may hold values from 0 to 31, as said below
- row_owners: int32 [8, 4, 32], P('pipe', 'tensor'), may hold values from 0 to 31, as said below
Outputs:
- grad_strips: bfloat16 [8, 4, 4096, 1024], P('pipe', 'tensor', 'dp')
The draws below stay inside these ranges and needn't reach their ends.
Inputs may be any that keep to these rules, and one draw needn't show every extreme that they name: `tile_picks`: for each section, replica and row group, the 16 picked row blocks j have distinct owners row_owners[p, u, j]; c is below 2. Each row_owners[p, u] is a permutation of 0 to 31.
All inputs are finite; a program needn't handle non-finite values.
Results may differ from the reference program's by a relative error of at most 0.001.
Values may be sent and summed in bfloat16 or wider, within the bound.
A program may use at most 32 MiB of HBM per device.

```python
import jax
import jax.numpy as jnp
from jax import lax

D = 16384
KV = 1024
TILE = 128
MICRO = 2
TOK_DEV = 128
TOKENS = 4096
SLOTS = 4
ROWB = 32
CBLK = 2
N_PIPE = 8
N_DP = 32
N_TENSOR = 4


def owner_table(key):
    row_count = D // (TILE * N_TENSOR)
    keys = jax.random.split(jax.random.fold_in(key, 11), N_PIPE * N_TENSOR)
    perms = jax.vmap(lambda single: jax.random.permutation(single, row_count))(keys)
    return perms.reshape(N_PIPE, N_TENSOR, row_count).astype(jnp.int32)


def draw_row_owners(key, part):
    return owner_table(key)


def draw_tile_picks(key, part):
    row_count = D // (TILE * N_TENSOR)
    owned = row_count // N_DP
    col_count = KV // (TILE * N_TENSOR)
    slot_count = max(1, N_DP // (2 * N_TENSOR))
    table = owner_table(key)
    inverse = jnp.argsort(table, axis=-1).astype(jnp.int32)
    keys = jax.random.split(jax.random.fold_in(key, 23), N_PIPE * N_DP * N_TENSOR)
    perms = jax.vmap(lambda single: jax.random.permutation(single, N_DP))(keys)
    perms = perms.reshape(N_PIPE, N_DP, N_TENSOR, N_DP)[..., :N_TENSOR * slot_count].astype(jnp.int32)
    within = jax.random.randint(jax.random.fold_in(key, 31), perms.shape, 0, owned).astype(jnp.int32)
    target = perms * owned + within
    spread = jnp.broadcast_to(inverse[:, None, :, :], (N_PIPE, N_DP, N_TENSOR, row_count))
    rows = jnp.take_along_axis(spread, target, axis=-1)
    shape = (N_PIPE, N_DP, N_TENSOR, N_TENSOR, slot_count)
    rows = rows.reshape(shape)
    cols = jax.random.randint(jax.random.fold_in(key, 47), shape, 0, col_count).astype(jnp.int32)
    return jnp.stack([rows, cols], axis=-1).astype(jnp.int32)


def level_of(stream_key, shape, cuts, least, largest):
    gain = 1.0
    for axis_at, parts in cuts:
        steps = jax.random.uniform(jax.random.fold_in(jax.random.fold_in(stream_key, 6), axis_at), (parts,), jnp.float32, least / len(cuts), largest / len(cuts))
        gain = gain * jnp.repeat(jnp.exp(steps), shape[axis_at] // parts).reshape((-1,) + (1,) * (len(shape) - 1 - axis_at))
    return gain


def noise(rng, extent, deviation, reach, cuts=(), held_as=jnp.bfloat16):
    array = deviation * jax.random.normal(rng, extent, jnp.float32)
    if cuts:
        array = array * level_of(rng, extent, cuts, -0.22, 0.18)
    return jnp.clip(array, -reach, reach).astype(held_as)


def setup_inputs(seed: int = 0) -> dict:
    key_of = jax.random.split(jax.random.key(seed), 6)
    activations = noise(key_of[0], (N_PIPE, MICRO, TOKENS, D), 1.0, 6.0, ((0, 8), (2, 32), (3, 4)))
    cotangent = noise(key_of[1], (N_PIPE, MICRO, TOKENS, KV), 0.0625, 0.5, ((0, 8), (2, 32), (3, 4)))
    error_tiles = noise(key_of[2], (N_PIPE, N_DP, N_TENSOR, N_TENSOR, SLOTS, TILE, TILE), 0.5, 4.0, ((0, 8), (1, 32), (2, 4)))
    tile_picks = draw_tile_picks(jax.random.fold_in(key_of[5], 71), 0)
    row_owners = draw_row_owners(jax.random.fold_in(key_of[5], 71), 0)
    return {"activations": activations, "cotangent": cotangent, "error_tiles": error_tiles, "tile_picks": tile_picks, "row_owners": row_owners}


def reference(activations, cotangent, error_tiles, tile_picks, row_owners):
    col_blocks = KV // TILE
    returned = jnp.roll(cotangent, -1, axis=0)
    dest_offset = (jnp.arange(N_TENSOR, dtype=jnp.int32) * ROWB)[:, None, None]
    source_offset = (jnp.arange(N_TENSOR, dtype=jnp.int32) * CBLK)[None, :, None]

    def one_section(section_index):
        section_acts = activations[section_index]
        section_grad = returned[section_index]

        def one_replica(running, replica):
            first_row = (replica * TOK_DEV).astype(jnp.int32)
            inputs = lax.dynamic_slice_in_dim(section_acts, first_row, TOK_DEV, 1).reshape(MICRO * TOK_DEV, D // TILE, TILE)
            outputs = lax.dynamic_slice_in_dim(section_grad, first_row, TOK_DEV, 1).reshape(MICRO * TOK_DEV, col_blocks, TILE)
            chosen = tile_picks[section_index, replica]
            row_index = (chosen[..., 0] + dest_offset).reshape(-1).astype(jnp.int32)
            col_index = (chosen[..., 1] + source_offset).reshape(-1).astype(jnp.int32)
            picked_in = jnp.take(inputs, row_index, axis=1).astype(jnp.float32)
            picked_out = jnp.take(outputs, col_index, axis=1).astype(jnp.float32)
            tile_sums = jnp.einsum('tmi,tmk->mik', picked_in, picked_out)
            carried = jnp.transpose(error_tiles[section_index, replica], (1, 0, 2, 3, 4)).reshape(-1, TILE, TILE).astype(jnp.float32)
            running = running.at[row_index, col_index].add(tile_sums + carried)
            return running, None

        dense_grad = jnp.zeros((D // TILE, col_blocks, TILE, TILE), jnp.float32)
        dense_grad, unused = lax.scan(one_replica, dense_grad, jnp.arange(N_DP, dtype=jnp.int32))
        dense_grad = dense_grad.reshape(N_TENSOR, ROWB, col_blocks, TILE, TILE)

        def reorder(stacked, ordering):
            return jnp.zeros_like(stacked).at[ordering].set(stacked)

        ordered = jax.vmap(reorder)(dense_grad, row_owners[section_index])
        return jnp.transpose(ordered, (0, 1, 3, 2, 4)).reshape(N_TENSOR, D // N_TENSOR, KV)

    result = lax.map(one_section, jnp.arange(N_PIPE, dtype=jnp.int32))
    return result.astype(jnp.bfloat16)
```

```python
import jax
import jax.numpy as jnp
from jax import lax
from jax.sharding import PartitionSpec as P


def passed_along(value, axis, steps):
    count = lax.axis_size(axis)
    pairs = [(source, (source + steps) % count) for source in range(count)]
    return lax.ppermute(value, axis, pairs)


def body(activations, cotangent, error_tiles, tile_picks, row_owners):
    tile_edge = error_tiles.shape[-1]
    tensor_count = lax.axis_size("tensor")
    replica_count = lax.axis_size("dp")
    replica_index = lax.axis_index("dp")
    returned = passed_along(cotangent, "pipe", -1)
    columns = lax.all_gather(returned, "tensor", axis=3, tiled=True)
    arrived = lax.all_to_all(error_tiles, "tensor", split_axis=3, concat_axis=2, tiled=True)
    width = columns.shape[-1]
    col_blocks = width // tile_edge
    group_blocks = col_blocks // tensor_count
    local_rows = activations.shape[-1] // tile_edge
    owned = local_rows // replica_count
    token_rows = activations.shape[1] * activations.shape[2]
    inputs = activations.reshape(token_rows, local_rows, tile_edge)
    outputs = columns.reshape(token_rows, col_blocks, tile_edge)
    every_pick = tile_picks[0, :, 0]
    source_offset = (jnp.arange(tensor_count, dtype=jnp.int32) * group_blocks)[None, :, None]
    pick_rows = every_pick[..., 0].reshape(replica_count, -1)
    pick_cols = (every_pick[..., 1] + source_offset).reshape(replica_count, -1)
    mine_rows = lax.dynamic_index_in_dim(pick_rows, replica_index, 0, keepdims=False)
    mine_cols = lax.dynamic_index_in_dim(pick_cols, replica_index, 0, keepdims=False)
    picked_in = jnp.take(inputs, mine_rows, axis=1)
    picked_out = jnp.take(outputs, mine_cols, axis=1)
    slot_total = mine_rows.shape[0]
    grads = jnp.einsum("tmi,tmk->mik", picked_in, picked_out, preferred_element_type=jnp.float32)
    grads = grads.reshape(slot_total, tile_edge * tile_edge)
    table = row_owners[0, 0]
    placed = jnp.sum(
        jnp.where(pick_rows[..., None] == jnp.arange(local_rows, dtype=jnp.int32), table, 0),
        axis=-1,
    )
    owner_index = placed // owned
    within_owner = placed % owned
    my_owner = lax.dynamic_index_in_dim(owner_index, replica_index, 0, keepdims=False)
    send_map = (my_owner[None, :] == jnp.arange(replica_count, dtype=jnp.int32)[:, None]).astype(
        jnp.float32
    )
    position = within_owner * col_blocks + pick_cols
    landing = (owner_index == replica_index)[..., None] & (
        position[..., None] == jnp.arange(owned * col_blocks, dtype=jnp.int32)
    )
    recv_map = jnp.transpose(jnp.sum(landing.astype(jnp.float32), axis=1))
    carried = arrived.reshape(slot_total, tile_edge * tile_edge).astype(jnp.float32)
    highest = lax.Precision.HIGHEST
    outgoing = jnp.dot(
        send_map, grads + carried, precision=highest, preferred_element_type=jnp.float32
    )
    outgoing = outgoing.reshape(replica_count, tile_edge, tile_edge)
    levels = 32767.0
    reach = jnp.maximum(jnp.max(jnp.abs(outgoing), axis=1, keepdims=True), 1e-30)
    codes = jnp.round(outgoing * (levels / reach)).astype(jnp.int16)
    codes = lax.all_to_all(codes, "dp", split_axis=0, concat_axis=0, tiled=True)
    steps = lax.all_to_all(
        reach * (1.0 / levels), "dp", split_axis=0, concat_axis=0, tiled=True
    )
    incoming = (codes.astype(jnp.float32) * steps).reshape(replica_count, -1)
    strip = jnp.dot(recv_map, incoming, precision=highest, preferred_element_type=jnp.float32)
    strip = strip.reshape(owned, col_blocks, tile_edge, tile_edge)
    strip = jnp.transpose(strip, (0, 2, 1, 3)).reshape(1, 1, owned * tile_edge, width)
    return strip.astype(jnp.bfloat16)


def solution(mesh):
    in_specs = (
        P("pipe", None, "dp", "tensor"),
        P("pipe", None, "dp", "tensor"),
        P("pipe", "dp", "tensor", None, None, None, None),
        P("pipe", None, "tensor", None, None, None),
        P("pipe", "tensor", None),
    )
    out_specs = P("pipe", "tensor", "dp", None)
    return jax.shard_map(body, mesh=mesh, in_specs=in_specs, out_specs=out_specs, check_vma=False)
```

```python
import functools

import jax
import jax.numpy as jnp
from jax import lax
from jax.experimental import pallas as pl
from jax.experimental.pallas import tpu as pltpu
from jax.sharding import PartitionSpec as P

MESH = pl.DeviceIdType.MESH
LEVELS = 32767.0


def peer(index, place, chips, way):
    half = chips // 2
    turn = index + 2
    distance = half - turn // 4
    edge = (distance == half) | (distance == 0)
    flip = jnp.where(edge, (turn + 1) % 2, (turn // 2) % 2)
    sign = jnp.where(turn % 2 == 0, way, -way)
    chip = lax.rem(place // 2 + sign * distance + 2 * chips, chips)
    core = lax.rem(place % 2 + flip, 2)
    return chip * 2 + core


def kernel(
    rows, cols, picks, marks, activations, cotangent, errors, strip,
    held_in, held_out, held_err, codes_out, steps_out, codes_in, steps_in, total,
    in_sem, own_sem, pipe_sems, error_sems, column_sems, code_sems, step_sems,
):
    pipe_count, replicas = lax.axis_size("pipe"), lax.axis_size("dp")
    groups = lax.axis_size("tensor")
    chips = replicas // 2
    section, place, group = lax.axis_index("pipe"), lax.axis_index("dp"), lax.axis_index("tensor")
    before, after = lax.rem(section + pipe_count - 1, pipe_count), lax.rem(section + 1, pipe_count)
    right, left = lax.rem(group + 1, groups), lax.rem(group + groups - 1, groups)
    far = lax.rem(group + 2, groups)
    micro, tokens, width = cotangent.shape
    edge = codes_out.shape[-1]
    slots = errors.shape[1]
    blocks = width // edge

    def load_in(block):
        span = pl.ds(pl.multiple_of(block * edge, edge), edge)
        return pltpu.make_async_copy(
            activations.at[:, :, span], held_in.at[block], in_sem.at[block]
        )

    @pl.loop(0, held_in.shape[0])
    def _(block):
        load_in(block).start()

    def err_slots(origin):
        return held_err.at[pl.ds(origin * slots, slots)]

    load_err = pltpu.make_async_copy(errors.at[group], err_slots(group), own_sem)
    load_err.start()

    barrier = pltpu.get_barrier_semaphore()
    for name, other in (
        ("tensor", right), ("tensor", left), ("tensor", far), ("pipe", before), ("pipe", after),
    ):
        pl.semaphore_signal(barrier, inc=1, device_id={name: other}, device_id_type=MESH)

    @pl.loop(1, replicas)
    def _(step):
        other = lax.rem(place + step, replicas)
        pl.semaphore_signal(barrier, inc=1, device_id={"dp": other}, device_id_type=MESH)

    pl.semaphore_wait(barrier, replicas + 4)

    def remote(source, target, sems, slot, device):
        return pltpu.make_async_remote_copy(
            src_ref=source, dst_ref=target,
            send_sem=sems.at[(0,) + slot], recv_sem=sems.at[(1,) + slot],
            device_id=device, device_id_type=MESH,
        )

    def columns(origin, part):
        return held_out.at[pl.ds(origin * blocks, blocks), part]

    pipe_copies = []
    for part in range(micro):
        for block in range(blocks):
            copy = remote(
                cotangent.at[part, :, pl.ds(block * edge, edge)],
                held_out.at[group * blocks + block, part],
                pipe_sems, (part, block), {"pipe": before},
            )
            copy.start()
            pipe_copies.append(copy)
    error_copies = []
    for slot, other in enumerate((right, left, far)):
        copy = remote(
            errors.at[other], err_slots(group), error_sems, (slot,), {"tensor": other}
        )
        copy.start()
        error_copies.append(copy)

    to_right, to_left, onward = [], [], []
    for part in range(micro):
        for block in range(blocks):
            pipe_copies[part * blocks + block].wait_recv()
        own = columns(group, part)
        copy = remote(own, own, column_sems, (0, part), {"tensor": right})
        copy.start()
        to_right.append(copy)
        copy = remote(own, own, column_sems, (1, part), {"tensor": left})
        copy.start()
        to_left.append(copy)
    for part in range(micro):
        if part % 2 == 0:
            to_left[part].wait_recv()
            piece = columns(right, part)
            copy = remote(piece, piece, column_sems, (2, part), {"tensor": left})
        else:
            to_right[part].wait_recv()
            piece = columns(left, part)
            copy = remote(piece, piece, column_sems, (2, part), {"tensor": right})
        copy.start()
        onward.append(copy)

    @pl.loop(0, held_in.shape[0])
    def _(block):
        load_in(block).wait()

    load_err.wait()
    for copy in error_copies:
        copy.wait_recv()
    for part in range(micro):
        if part % 2 == 0:
            to_right[part].wait_recv()
        else:
            to_left[part].wait_recv()
    for copy in onward:
        copy.wait_recv()

    def exchange(index):
        other = peer(index, place, chips, 1)
        return (
            remote(codes_out.at[index], codes_in.at[index], code_sems, (index,), {"dp": other}),
            remote(steps_out.at[index], steps_in.at[index], step_sems, (index,), {"dp": other}),
        )

    def make_tile(index):
        other = peer(index, place, chips, 1)
        source = held_in[rows[other]].reshape(micro * tokens, edge)
        sink = held_out[cols[other]].reshape(micro * tokens, edge)
        tile = lax.dot_general(
            source, sink, (((0,), (0,)), ((), ())), preferred_element_type=jnp.float32
        )
        tile = tile + held_err[picks[other]].astype(jnp.float32)
        reach = jnp.maximum(jnp.max(jnp.abs(tile), axis=0, keepdims=True), 1e-30)
        codes = jnp.round(tile * (LEVELS / reach)).astype(jnp.int32)
        codes_out[index] = codes.astype(jnp.int16)
        steps_out[index] = reach * (1.0 / LEVELS)

    make_tile(0)

    @pl.loop(1, replicas)
    def _(index):
        make_tile(index)
        for copy in exchange(index - 1):
            copy.start()

    total[...] = jnp.zeros_like(total)

    def add_tile(index, codes, steps):
        mark = marks[peer(index, place, chips, -1)]
        value = codes[index].astype(jnp.int32).astype(jnp.float32) * steps[index]
        for block in range(total.shape[0]):
            total[block] += value * mark[block : block + 1]

    add_tile(replicas - 1, codes_out, steps_out)

    @pl.loop(0, replicas - 1)
    def _(index):
        for copy in exchange(index):
            copy.wait_recv()
        add_tile(index, codes_in, steps_in)

    for block in range(total.shape[0]):
        strip[:, pl.ds(block * edge, edge)] = total[block].astype(strip.dtype)

    for copy in pipe_copies + error_copies + to_right + to_left + onward:
        copy.wait_send()

    @pl.loop(0, replicas - 1)
    def _(index):
        for copy in exchange(index):
            copy.wait_send()


def tables(tile_picks, row_owners, blocks, lanes):
    replicas = tile_picks.shape[1]
    place = lax.axis_index("dp")
    groups, slots = tile_picks.shape[3:5]
    rows = tile_picks[0, :, 0, :, :, 0].reshape(replicas, groups * slots)
    offset = (jnp.arange(groups * slots, dtype=jnp.int32) // slots) * blocks
    cols = tile_picks[0, :, 0, :, :, 1].reshape(replicas, groups * slots) + offset
    owners = row_owners[0, 0]
    count = owners.shape[0]
    mine_rows = lax.dynamic_index_in_dim(rows, place, 0, keepdims=False)
    mine_cols = lax.dynamic_index_in_dim(cols, place, 0, keepdims=False)
    numbers = jnp.arange(count, dtype=jnp.int32)
    row_of = jnp.sum(jnp.where(owners[None, :] == numbers[:, None], numbers[None, :], 0), axis=1)
    picked = mine_rows[None, :] == row_of[:, None]
    numbers16 = jnp.arange(groups * slots, dtype=jnp.int32)

    def chosen(values):
        return jnp.sum(jnp.where(picked, values[None, :], 0), axis=1)

    my_row = jnp.sum(jnp.where(owners == place, numbers, 0))
    columns = jnp.arange(groups * blocks, dtype=jnp.int32)
    here = (rows == my_row)[..., None] & (cols[..., None] == columns)
    marks = jnp.sum(here.astype(jnp.float32), axis=1)
    marks = jnp.broadcast_to(marks[..., None], marks.shape + (lanes,))
    return chosen(mine_rows), chosen(mine_cols), chosen(numbers16), marks


def body(activations, cotangent, error_tiles, tile_picks, row_owners):
    edge = error_tiles.shape[-1]
    groups, replicas = lax.axis_size("tensor"), lax.axis_size("dp")
    micro, tokens, features = activations.shape[1:]
    width = cotangent.shape[-1]
    slots = error_tiles.shape[4]
    rows, cols, picks, marks = tables(tile_picks, row_owners, width // edge, edge)
    hbm = pl.BlockSpec(memory_space=pl.ANY)
    vmem, smem = pl.BlockSpec(memory_space=pltpu.VMEM), pl.BlockSpec(memory_space=pltpu.SMEM)
    dma = pltpu.SemaphoreType.DMA
    strip = pl.pallas_call(
        kernel,
        out_shape=jax.ShapeDtypeStruct((edge, groups * width), jnp.bfloat16),
        in_specs=[smem, smem, smem, vmem, hbm, hbm, hbm],
        out_specs=vmem,
        scratch_shapes=[
            pltpu.VMEM((features // edge, micro, tokens, edge), jnp.bfloat16),
            pltpu.VMEM((groups * width // edge, micro, tokens, edge), jnp.bfloat16),
            pltpu.VMEM((groups * slots, edge, edge), jnp.bfloat16),
            pltpu.VMEM((replicas, edge, edge), jnp.int16),
            pltpu.VMEM((replicas, 1, edge), jnp.float32),
            pltpu.VMEM((replicas, edge, edge), jnp.int16),
            pltpu.VMEM((replicas, 1, edge), jnp.float32),
            pltpu.VMEM((groups * width // edge, edge, edge), jnp.float32),
            dma((features // edge,)), dma(()), dma((2, micro, width // edge)),
            dma((2, 3)), dma((2, 3, micro)),
            dma((2, replicas)), dma((2, replicas)),
        ],
        compiler_params=pltpu.CompilerParams(
            collective_id=0, has_side_effects=True, vmem_limit_bytes=60 << 20
        ),
    )(
        rows, cols, picks, marks,
        activations.reshape(micro, tokens, features),
        cotangent.reshape(micro, tokens, width),
        error_tiles.reshape(groups, slots, edge, edge),
    )
    return strip.reshape(1, 1, edge, groups * width)


def solution(mesh):
    in_specs = (
        P("pipe", None, "dp", "tensor"),
        P("pipe", None, "dp", "tensor"),
        P("pipe", "dp", "tensor", None, None, None, None),
        P("pipe", None, "tensor", None, None, None),
        P("pipe", "tensor", None),
    )
    out_specs = P("pipe", "tensor", "dp", None)
    return jax.shard_map(body, mesh=mesh, in_specs=in_specs, out_specs=out_specs, check_vma=False)
```

```python
import jax
import jax.numpy as jnp
from jax import lax
from jax.experimental import pallas as pl
from jax.experimental.pallas import tpu as pltpu
from jax.sharding import PartitionSpec as P

MESH = pl.DeviceIdType.MESH
LEVELS = 32767.0


def hit(left, right):
    apart = left - right
    return 1 - jnp.minimum(apart * apart, 1)


def peer(index, place, chips, way):
    half = chips // 2
    turn = index + 2
    distance = half - turn // 4
    edge = (distance == half) | (distance == 0)
    flip = jnp.where(edge, (turn + 1) % 2, (turn // 2) % 2)
    sign = jnp.where(turn % 2 == 0, way, -way)
    chip = lax.rem(place // 2 + sign * distance + 2 * chips, chips)
    core = lax.rem(place % 2 + flip, 2)
    return chip * 2 + core


def kernel(
    picks, pick_scalars, owners, activations, cotangent, errors, strip,
    held_in, held_out, held_err, codes_out, steps_out, codes_in, steps_in, listed, table,
    in_sem, own_sem, table_sem, pipe_sems, error_sems, column_sems, code_sems, step_sems, near_sems,
):
    pipe_count, replicas = lax.axis_size("pipe"), lax.axis_size("dp")
    groups = lax.axis_size("tensor")
    chips = replicas // 2
    section, place, group = lax.axis_index("pipe"), lax.axis_index("dp"), lax.axis_index("tensor")
    before, after = lax.rem(section + pipe_count - 1, pipe_count), lax.rem(section + 1, pipe_count)
    right, left = lax.rem(group + 1, groups), lax.rem(group + groups - 1, groups)
    far = lax.rem(group + 2, groups)
    micro, tokens, width = cotangent.shape
    edge = codes_out.shape[-1]
    slots = errors.shape[1]
    blocks = width // edge

    def load_in(block):
        span = pl.ds(pl.multiple_of(block * edge, edge), edge)
        return pltpu.make_async_copy(
            activations.at[:, :, span], held_in.at[block], in_sem.at[block]
        )

    @pl.loop(0, held_in.shape[0])
    def _(block):
        load_in(block).start()

    def err_slots(origin):
        return held_err.at[pl.ds(origin * slots, slots)]

    load_err = pltpu.make_async_copy(errors.at[group], err_slots(group), own_sem)
    load_err.start()

    barrier = pltpu.get_barrier_semaphore()
    for name, other in (
        ("tensor", right), ("tensor", left), ("tensor", far), ("pipe", before), ("pipe", after),
    ):
        pl.semaphore_signal(barrier, inc=1, device_id={name: other}, device_id_type=MESH)

    chip, core = place // 2, place % 2

    def replica(shift, which):
        return lax.rem(chip + shift + chips, chips) * 2 + which

    near = [replica(shift, which) for shift in (1, -1) for which in (0, 1)]
    for other in near + [replica(0, 1 - core)]:
        pl.semaphore_signal(barrier, inc=1, device_id={"dp": other}, device_id_type=MESH)

    rows = held_in.shape[0]
    picked = groups * slots
    lanes = lax.broadcasted_iota(jnp.int32, (1, replicas), 1)
    row_of = jnp.zeros((1, replicas), jnp.int32)
    my_row = 0
    for row in range(rows):
        row_of += hit(lanes, owners[row]) * row
        my_row += hit(owners[row], place) * row
    sends = jnp.zeros((1, replicas), jnp.int32)
    hears = jnp.zeros((1, replicas), jnp.int32)
    for pick in range(picked):
        at = pick // slots, pick % slots
        row = pick_scalars[at + (0, place)]
        column = pick_scalars[at + (1, place)] + at[0] * blocks
        sends += hit(row_of, row) * ((row * groups * blocks + column) * picked + pick)
        hears += hit(picks[at + (pl.ds(0, 1),)], my_row) * (
            picks[at + (pl.ds(1, 1),)] + (at[0] * blocks + 1)
        )
    listed[0:1, 0:replicas] = sends
    listed[1:2, 0:replicas] = hears - 1

    pl.semaphore_wait(barrier, 10)

    def remote(source, target, sems, slot, device):
        return pltpu.make_async_remote_copy(
            src_ref=source, dst_ref=target,
            send_sem=sems.at[(0,) + slot], recv_sem=sems.at[(1,) + slot],
            device_id=device, device_id_type=MESH,
        )

    def columns(origin, part):
        return held_out.at[pl.ds(origin * blocks, blocks), part]

    pipe_copies = []
    for part in range(micro):
        for block in range(blocks):
            copy = remote(
                cotangent.at[part, :, pl.ds(block * edge, edge)],
                held_out.at[group * blocks + block, part],
                pipe_sems, (part, block), {"pipe": before},
            )
            copy.start()
            pipe_copies.append(copy)
    error_copies = []
    for slot, other in enumerate((right, left, far)):
        copy = remote(
            errors.at[other], err_slots(group), error_sems, (slot,), {"tensor": other}
        )
        copy.start()
        error_copies.append(copy)

    load_table = pltpu.make_async_copy(listed, table, table_sem)
    load_table.start()

    def meet(number):
        distance = 2**number
        for way, shift in enumerate((distance, -distance)):
            for which in (0, 1):
                pl.semaphore_signal(
                    near_sems.at[number, way * 2 + core], inc=1,
                    device_id={"dp": replica(shift, which)}, device_id_type=MESH,
                )
        for slot in range(4):
            pl.semaphore_wait(near_sems.at[number, slot], 1)

    meetings = near_sems.shape[0]
    early = meetings - 1
    for number in range(early):
        meet(number)

    to_right, to_left, onward = [], [], []
    for part in range(micro):
        for block in range(blocks):
            pipe_copies[part * blocks + block].wait_recv()
        own = columns(group, part)
        copy = remote(own, own, column_sems, (0, part), {"tensor": right})
        copy.start()
        to_right.append(copy)
        copy = remote(own, own, column_sems, (1, part), {"tensor": left})
        copy.start()
        to_left.append(copy)
    for number in range(early, meetings):
        meet(number)
    for part in range(micro):
        if part % 2 == 0:
            to_left[part].wait_recv()
            piece = columns(right, part)
            copy = remote(piece, piece, column_sems, (2, part), {"tensor": left})
        else:
            to_right[part].wait_recv()
            piece = columns(left, part)
            copy = remote(piece, piece, column_sems, (2, part), {"tensor": right})
        copy.start()
        onward.append(copy)

    @pl.loop(0, held_in.shape[0])
    def _(block):
        load_in(block).wait()

    load_err.wait()
    load_table.wait()
    for copy in error_copies:
        copy.wait_recv()
    for part in range(micro):
        if part % 2 == 0:
            to_right[part].wait_recv()
        else:
            to_left[part].wait_recv()
    for copy in onward:
        copy.wait_recv()

    def exchange(index):
        other = peer(index, place, chips, 1)
        return (
            remote(codes_out.at[index], codes_in.at[index], code_sems, (index,), {"dp": other}),
            remote(steps_out.at[index], steps_in.at[index], step_sems, (index,), {"dp": other}),
        )

    def make_tile(index):
        entry = table[0, peer(index, place, chips, 1)]
        pick, entry = lax.rem(entry, picked), lax.div(entry, picked)
        column, row = lax.rem(entry, groups * blocks), lax.div(entry, groups * blocks)
        source = held_in[row].reshape(micro * tokens, edge)
        sink = held_out[column].reshape(micro * tokens, edge)
        tile = lax.dot_general(
            source, sink, (((0,), (0,)), ((), ())), preferred_element_type=jnp.float32
        )
        tile = tile + held_err[pick].astype(jnp.float32)
        reach = jnp.maximum(jnp.max(jnp.abs(tile), axis=0, keepdims=True), 1e-30)
        codes = jnp.round(tile * (LEVELS / reach)).astype(jnp.int32)
        codes_out[index] = codes.astype(jnp.int16)
        steps_out[index] = reach * (1.0 / LEVELS)

    make_tile(0)

    @pl.loop(1, replicas)
    def _(index):
        make_tile(index)
        for copy in exchange(index - 1):
            copy.start()

    strip[...] = jnp.zeros_like(strip)
    columns_at = lax.broadcasted_iota(jnp.int32, (groups * blocks, edge), 0)

    def add_tile(index, codes, steps):
        mark = hit(columns_at, table[1, peer(index, place, chips, -1)]).astype(jnp.float32)
        value = codes[index].astype(jnp.int32).astype(jnp.float32) * steps[index]
        for block in range(groups * blocks):
            strip[:, pl.ds(block * edge, edge)] += value * mark[block : block + 1]

    add_tile(replicas - 1, codes_out, steps_out)

    @pl.loop(0, replicas - 1)
    def _(index):
        for copy in exchange(index):
            copy.wait_recv()
        add_tile(index, codes_in, steps_in)

    for copy in pipe_copies + error_copies + to_right + to_left + onward:
        copy.wait_send()

    @pl.loop(0, replicas - 1)
    def _(index):
        for copy in exchange(index):
            copy.wait_send()


def body(activations, cotangent, error_tiles, tile_picks, row_owners):
    edge = error_tiles.shape[-1]
    groups, replicas = lax.axis_size("tensor"), lax.axis_size("dp")
    micro, tokens, features = activations.shape[1:]
    width = cotangent.shape[-1]
    slots = error_tiles.shape[4]
    picks = jnp.transpose(tile_picks[0, :, 0], (1, 2, 3, 0))
    meetings = max(1, (replicas // 2 - 1).bit_length()) - 1
    hbm = pl.BlockSpec(memory_space=pl.ANY)
    vmem, smem = pl.BlockSpec(memory_space=pltpu.VMEM), pl.BlockSpec(memory_space=pltpu.SMEM)
    dma = pltpu.SemaphoreType.DMA
    strip = pl.pallas_call(
        kernel,
        out_shape=jax.ShapeDtypeStruct((edge, groups * width), jnp.float32),
        in_specs=[vmem, smem, smem, hbm, hbm, hbm],
        out_specs=vmem,
        scratch_shapes=[
            pltpu.VMEM((features // edge, micro, tokens, edge), jnp.bfloat16),
            pltpu.VMEM((groups * width // edge, micro, tokens, edge), jnp.bfloat16),
            pltpu.VMEM((groups * slots, edge, edge), jnp.bfloat16),
            pltpu.VMEM((replicas, edge, edge), jnp.int16),
            pltpu.VMEM((replicas, 1, edge), jnp.float32),
            pltpu.VMEM((replicas, edge, edge), jnp.int16),
            pltpu.VMEM((replicas, 1, edge), jnp.float32),
            pltpu.VMEM((2, 128), jnp.int32),
            pltpu.SMEM((2, 128), jnp.int32),
            dma((features // edge,)), dma(()), dma(()), dma((2, micro, width // edge)),
            dma((2, 3)), dma((2, 3, micro)),
            dma((2, replicas)), dma((2, replicas)),
            pltpu.SemaphoreType.REGULAR((max(1, meetings), 4)),
        ],
        compiler_params=pltpu.CompilerParams(
            collective_id=0, has_side_effects=True, vmem_limit_bytes=60 << 20
        ),
    )(
        picks, picks, row_owners[0, 0],
        activations.reshape(micro, tokens, features),
        cotangent.reshape(micro, tokens, width),
        error_tiles.reshape(groups, slots, edge, edge),
    )
    return strip.astype(jnp.bfloat16).reshape(1, 1, edge, groups * width)


def solution(mesh):
    in_specs = (
        P("pipe", None, "dp", "tensor"),
        P("pipe", None, "dp", "tensor"),
        P("pipe", "dp", "tensor", None, None, None, None),
        P("pipe", None, "tensor", None, None, None),
        P("pipe", "tensor", None),
    )
    out_specs = P("pipe", "tensor", "dp", None)
    return jax.shard_map(body, mesh=mesh, in_specs=in_specs, out_specs=out_specs, check_vma=False)
```

```python
import jax
import jax.numpy as jnp
from jax import lax
from jax.experimental import pallas as pl
from jax.experimental.pallas import tpu as pltpu
from jax.sharding import PartitionSpec as P

MESH = pl.DeviceIdType.MESH
LEVELS = 32767.0
RELAY = 2


def hit(left, right):
    apart = left - right
    return 1 - jnp.minimum(apart * apart, 1)


def kernel(
    picks, pick_scalars, owners, activations, cotangent, errors, strip,
    held_in, held_out, held_err, passing, codes_out, steps_out, codes_in, steps_in, sums, listed,
    table, in_sem, own_sem, table_sem, pipe_sems, error_sems, column_sems,
    code_send, code_recv, step_send, step_recv, near_sems,
):
    pipe_count, replicas = lax.axis_size("pipe"), lax.axis_size("dp")
    groups = lax.axis_size("tensor")
    chips = replicas // 2
    section, place, group = lax.axis_index("pipe"), lax.axis_index("dp"), lax.axis_index("tensor")
    before, after = lax.rem(section + pipe_count - 1, pipe_count), lax.rem(section + 1, pipe_count)
    right, left = lax.rem(group + 1, groups), lax.rem(group + groups - 1, groups)
    far = lax.rem(group + 2, groups)
    micro, tokens, width = cotangent.shape
    edge = codes_out.shape[-1]
    slots = errors.shape[1]
    blocks = width // edge

    def load_in(block):
        span = pl.ds(pl.multiple_of(block * edge, edge), edge)
        return pltpu.make_async_copy(
            activations.at[:, :, span], held_in.at[block], in_sem.at[block]
        )

    @pl.loop(0, held_in.shape[0])
    def _(block):
        load_in(block).start()

    picked = groups * slots
    first = slots // 2

    def err_slots(origin, start=0, count=slots):
        return held_err.at[pl.ds(origin * slots + start, count)]

    load_err = pltpu.make_async_copy(errors.at[group], err_slots(group), own_sem)
    load_err.start()

    barrier = pltpu.get_barrier_semaphore()
    for name, other in (
        ("tensor", right), ("tensor", left), ("tensor", far), ("pipe", before), ("pipe", after),
    ):
        pl.semaphore_signal(barrier, inc=1, device_id={name: other}, device_id_type=MESH)

    chip, core = place // 2, place % 2

    def replica(shift, which):
        return lax.rem(chip + shift + chips, chips) * 2 + which

    near = [replica(shift, which) for shift in (1, -1) for which in (0, 1)]
    for other in near + [replica(0, 1 - core)]:
        pl.semaphore_signal(barrier, inc=1, device_id={"dp": other}, device_id_type=MESH)

    pl.semaphore_wait(barrier, 10)

    def remote(source, target, sems, slot, device):
        return pltpu.make_async_remote_copy(
            src_ref=source, dst_ref=target,
            send_sem=sems.at[(0,) + slot], recv_sem=sems.at[(1,) + slot],
            device_id=device, device_id_type=MESH,
        )

    def columns(origin, part):
        return held_out.at[pl.ds(origin * blocks, blocks), part]

    pipe_copies = []
    for part in range(micro):
        for block in range(blocks):
            copy = remote(
                cotangent.at[part, :, pl.ds(block * edge, edge)],
                held_out.at[group * blocks + block, part],
                pipe_sems, (part, block), {"pipe": before},
            )
            copy.start()
            pipe_copies.append(copy)
    error_copies, through = [], []
    spans = (0, first), (first, slots - first)
    for way, other in enumerate((right, left)):
        start, count = spans[way]
        copy = remote(
            errors.at[far, pl.ds(start, count)], passing.at[pl.ds(start, count)],
            error_sems, (way,), {"tensor": other},
        )
        copy.start()
        through.append(copy)
    for way, other in enumerate((right, left)):
        copy = remote(
            errors.at[other], err_slots(group), error_sems, (2 + way,), {"tensor": other}
        )
        copy.start()
        error_copies.append(copy)

    def list_tables():
        lanes = lax.broadcasted_iota(jnp.int32, (1, replicas), 1)
        row_of = jnp.zeros((1, replicas), jnp.int32)
        owned = [place, replica(RELAY, core), replica(-RELAY, core)]
        wanted = [0 for _ in owned]
        for row in range(held_in.shape[0]):
            row_of += hit(lanes, owners[row]) * row
            wanted = [was + hit(owners[row], who) * row for was, who in zip(wanted, owned)]
        sends = jnp.zeros((1, replicas), jnp.int32)
        hears = [jnp.zeros((1, replicas), jnp.int32) for _ in owned]
        for pick in range(picked):
            at = pick // slots, pick % slots
            row = pick_scalars[at + (0, place)]
            column = pick_scalars[at + (1, place)] + at[0] * blocks
            sends += hit(row_of, row) * ((row * groups * blocks + column) * picked + pick)
            every_row = picks[at + (pl.ds(0, 1),)]
            every_column = picks[at + (pl.ds(1, 1),)] + (at[0] * blocks + 1)
            hears = [was + hit(every_row, row) * every_column for was, row in zip(hears, wanted)]
        listed[0:1, 0:replicas] = sends
        for number, columns in enumerate(hears):
            listed[number + 1 : number + 2, 0:replicas] = columns - 1

    def meet(number):
        distance = 2**number
        for way, shift in enumerate((distance, -distance)):
            for which in (0, 1):
                pl.semaphore_signal(
                    near_sems.at[number, way * 2 + core], inc=1,
                    device_id={"dp": replica(shift, which)}, device_id_type=MESH,
                )
        for slot in range(4):
            pl.semaphore_wait(near_sems.at[number, slot], 1)

    meetings = near_sems.shape[0]
    early = meetings - 1
    list_tables()
    for number in range(early):
        meet(number)
    load_table = pltpu.make_async_copy(listed, table, table_sem)
    load_table.start()
    for way, (origin, other) in enumerate(((left, right), (right, left))):
        start, count = spans[way]
        through[way].wait_recv()
        copy = remote(
            passing.at[pl.ds(start, count)], err_slots(origin, start, count),
            error_sems, (4 + way,), {"tensor": other},
        )
        copy.start()
        error_copies.append(copy)

    to_right, to_left, onward = [], [], []
    for part in range(micro):
        for block in range(blocks):
            pipe_copies[part * blocks + block].wait_recv()
        own = columns(group, part)
        copy = remote(own, own, column_sems, (0, part), {"tensor": right})
        copy.start()
        to_right.append(copy)
        copy = remote(own, own, column_sems, (1, part), {"tensor": left})
        copy.start()
        to_left.append(copy)
    for number in range(early, meetings):
        meet(number)
    for part in range(micro):
        if part % 2 == 0:
            to_left[part].wait_recv()
            piece = columns(right, part)
            copy = remote(piece, piece, column_sems, (2, part), {"tensor": left})
        else:
            to_right[part].wait_recv()
            piece = columns(left, part)
            copy = remote(piece, piece, column_sems, (2, part), {"tensor": right})
        copy.start()
        onward.append(copy)

    @pl.loop(0, held_in.shape[0])
    def _(block):
        load_in(block).wait()

    load_err.wait()
    load_table.wait()
    for copy in error_copies:
        copy.wait_recv()
    for part in range(micro):
        if part % 2 == 0:
            to_right[part].wait_recv()
        else:
            to_left[part].wait_recv()
    for copy in onward:
        copy.wait_recv()

    half = chips // 2
    gathered = 2 * (half - RELAY) - 1
    relayed = 2 * gathered
    direct_in = 2 * (gathered + 1)
    strips_in = direct_in + 5
    strips_out = replicas
    width_all = groups * blocks

    def post(source, target, device):
        return [
            pltpu.make_async_remote_copy(
                src_ref=out.at[source], dst_ref=into.at[target],
                send_sem=send.at[source], recv_sem=recv.at[target],
                device_id={"dp": device}, device_id_type=MESH,
            )
            for out, into, send, recv in (
                (codes_out, codes_in, code_send, code_recv),
                (steps_out, steps_in, step_send, step_recv),
            )
        ]

    def far_tile(index):
        turn = index + 2
        distance = half - turn // 4
        across = distance == half
        flip = jnp.where(across, turn % 2, (turn // 2) % 2)
        side = jnp.where(across, core, turn % 2)
        way = 1 - 2 * side
        which = lax.rem(core + flip, 2)
        slot = jnp.where(across, 0, 1 + (half - 1 - distance) * 2 + flip)
        return (
            replica(way * distance, which), replica(way * (distance - RELAY), which),
            side * (gathered + 1) + slot,
        )

    near_tiles = []
    for side, way in enumerate((1, -1)):
        near_tiles.append((
            replica(way * RELAY, 1 - core), replica(0, 1 - core), side * (gathered + 1) + gathered
        ))
    for side, way in enumerate((1, -1)):
        near_tiles.append((replica(way * RELAY, core), None, None))
    for flip in (0, 1):
        for side, way in enumerate((1, -1)):
            which = lax.rem(core + flip, 2)
            other = replica(way, which)
            near_tiles.append((other, other, direct_in + side * 2 + flip))
    other = replica(0, 1 - core)
    near_tiles.append((other, other, direct_in + 4))
    near_tiles.append((place, None, None))
    kept = relayed + 2

    def encode(value, slot):
        reach = jnp.maximum(jnp.max(jnp.abs(value), axis=0, keepdims=True), 1e-30)
        codes = jnp.round(value * (LEVELS / reach)).astype(jnp.int32)
        codes_out[slot] = codes.astype(jnp.int16)
        steps_out[slot] = reach * (1.0 / LEVELS)

    def decode(codes, steps, slot):
        return codes[slot].astype(jnp.int32).astype(jnp.float32) * steps[slot]

    def make_tile(index, target):
        entry = table[0, target]
        pick, entry = lax.rem(entry, picked), lax.div(entry, picked)
        column, row = lax.rem(entry, width_all), lax.div(entry, width_all)
        source = held_in[row].reshape(micro * tokens, edge)
        sink = held_out[column].reshape(micro * tokens, edge)
        tile = lax.dot_general(
            source, sink, (((0,), (0,)), ((), ())), preferred_element_type=jnp.float32
        )
        encode(tile + held_err[pick].astype(jnp.float32), index)

    def send_far(index):
        _, gatherer, slot = far_tile(index)
        return post(index, slot, gatherer)

    make_tile(0, far_tile(0)[0])

    @pl.loop(1, relayed)
    def _(index):
        make_tile(index, far_tile(index)[0])
        for copy in send_far(index - 1):
            copy.start()

    waiting = send_far(relayed - 1)
    sent = []
    for number, (target, device, slot) in enumerate(near_tiles):
        make_tile(relayed + number, target)
        for copy in waiting:
            copy.start()
        waiting = post(relayed + number, slot, device) if slot is not None else []
        sent += waiting
    for copy in waiting:
        copy.start()

    columns_at = lax.broadcasted_iota(jnp.int32, (width_all, edge), 0)
    sums[...] = jnp.zeros_like(sums)

    def await_slot(slot):
        for copy in post(0, slot, place):
            copy.wait_recv()

    def add_tile(number, source, codes, steps, slot):
        mark = hit(columns_at, table[1 + number, source]).astype(jnp.float32)
        value = decode(codes, steps, slot)
        for block in range(width_all):
            sums[number, :, pl.ds(block * edge, edge)] += value * mark[block : block + 1]

    sides = (1, 0), (2, 1)
    for number, side in sides:
        add_tile(number, place, codes_out, steps_out, kept + side)
        slot = side * (gathered + 1) + gathered
        await_slot(slot)
        add_tile(number, replica(0, 1 - core), codes_in, steps_in, slot)
    for number, side in sides:
        slot = side * (gathered + 1)
        await_slot(slot)
        source = replica((2 * side - 1) * (half - RELAY), side)
        add_tile(number, source, codes_in, steps_in, slot)

    @pl.loop(0, gathered - 1)
    def _(index):
        distance = half - 1 - index // 2
        which = lax.rem(core + index % 2, 2)
        for number, side in sides:
            slot = side * (gathered + 1) + 1 + index
            await_slot(slot)
            source = replica((2 * side - 1) * (distance - RELAY), which)
            add_tile(number, source, codes_in, steps_in, slot)

    waiting = []
    for block in range(width_all):
        for number, side in sides:
            spot = side * width_all + block
            encode(sums[number, :, pl.ds(block * edge, edge)], strips_out + spot)
            for copy in waiting:
                copy.start()
            device = replica((1 - 2 * side) * RELAY, core)
            waiting = post(strips_out + spot, strips_in + spot, device)
            sent += waiting
    for copy in waiting:
        copy.start()

    add_tile(0, place, codes_out, steps_out, replicas - 1)
    await_slot(direct_in + 4)
    add_tile(0, replica(0, 1 - core), codes_in, steps_in, direct_in + 4)
    for flip in (0, 1):
        for side in (0, 1):
            slot = direct_in + side * 2 + flip
            await_slot(slot)
            source = replica(2 * side - 1, lax.rem(core + flip, 2))
            add_tile(0, source, codes_in, steps_in, slot)
    for block in range(width_all):
        span = pl.ds(block * edge, edge)
        value = sums[0, :, span]
        for side in (0, 1):
            slot = strips_in + side * width_all + block
            await_slot(slot)
            value = value + decode(codes_in, steps_in, slot)
        strip[:, span] = value.astype(strip.dtype)

    for copy in pipe_copies + through + error_copies + to_right + to_left + onward + sent:
        copy.wait_send()

    @pl.loop(0, relayed)
    def _(index):
        for copy in send_far(index):
            copy.wait_send()


def body(activations, cotangent, error_tiles, tile_picks, row_owners):
    edge = error_tiles.shape[-1]
    groups, replicas = lax.axis_size("tensor"), lax.axis_size("dp")
    micro, tokens, features = activations.shape[1:]
    width = cotangent.shape[-1]
    slots = error_tiles.shape[4]
    picks = jnp.transpose(tile_picks[0, :, 0], (1, 2, 3, 0))
    strips = 2 * groups * width // edge
    outbox = replicas + strips
    inbox = 4 * (replicas // 4 - RELAY) + 5 + strips
    meetings = max(1, (replicas // 2 - 1).bit_length()) - 1
    hbm = pl.BlockSpec(memory_space=pl.ANY)
    vmem, smem = pl.BlockSpec(memory_space=pltpu.VMEM), pl.BlockSpec(memory_space=pltpu.SMEM)
    dma = pltpu.SemaphoreType.DMA
    strip = pl.pallas_call(
        kernel,
        out_shape=jax.ShapeDtypeStruct((edge, groups * width), jnp.bfloat16),
        in_specs=[vmem, smem, smem, hbm, hbm, hbm],
        out_specs=vmem,
        scratch_shapes=[
            pltpu.VMEM((features // edge, micro, tokens, edge), jnp.bfloat16),
            pltpu.VMEM((groups * width // edge, micro, tokens, edge), jnp.bfloat16),
            pltpu.VMEM((groups * slots, edge, edge), jnp.bfloat16),
            pltpu.VMEM((slots, edge, edge), jnp.bfloat16),
            pltpu.VMEM((outbox, edge, edge), jnp.int16),
            pltpu.VMEM((outbox, 1, edge), jnp.float32),
            pltpu.VMEM((inbox, edge, edge), jnp.int16),
            pltpu.VMEM((inbox, 1, edge), jnp.float32),
            pltpu.VMEM((3, edge, groups * width), jnp.float32),
            pltpu.VMEM((4, 128), jnp.int32),
            pltpu.SMEM((4, 128), jnp.int32),
            dma((features // edge,)), dma(()), dma(()), dma((2, micro, width // edge)),
            dma((2, 6)), dma((2, 3, micro)),
            dma((outbox,)), dma((inbox,)), dma((outbox,)), dma((inbox,)),
            pltpu.SemaphoreType.REGULAR((max(1, meetings), 4)),
        ],
        compiler_params=pltpu.CompilerParams(
            collective_id=0, has_side_effects=True, vmem_limit_bytes=60 << 20
        ),
    )(
        picks, picks, row_owners[0, 0],
        activations.reshape(micro, tokens, features),
        cotangent.reshape(micro, tokens, width),
        error_tiles.reshape(groups, slots, edge, edge),
    )
    return strip.reshape(1, 1, edge, groups * width)


def solution(mesh):
    in_specs = (
        P("pipe", None, "dp", "tensor"),
        P("pipe", None, "dp", "tensor"),
        P("pipe", "dp", "tensor", None, None, None, None),
        P("pipe", None, "tensor", None, None, None),
        P("pipe", "tensor", None),
    )
    out_specs = P("pipe", "tensor", "dp", None)
    return jax.shard_map(body, mesh=mesh, in_specs=in_specs, out_specs=out_specs, check_vma=False)
```

```python
import jax
import jax.numpy as jnp
from jax import lax
from jax.experimental import pallas as pl
from jax.experimental.pallas import tpu as pltpu
from jax.sharding import PartitionSpec as P

MESH = pl.DeviceIdType.MESH
LEVELS = 32767.0
RELAY = 2


def hit(left, right):
    apart = left - right
    return 1 - jnp.minimum(apart * apart, 1)


def kernel(
    all_picks, all_owners, activations, cotangent, errors, strip,
    picks, pick_scalars, owners, rounded,
    held_in, held_out, held_err, passing, codes_out, steps_out, codes_in, steps_in, sums, listed,
    table, list_sems, out_sems, in_sem, own_sem, table_sem, pipe_sems, error_sems, column_sems,
    code_send, code_recv, step_send, step_recv, near_sems,
):
    pipe_count, replicas = lax.axis_size("pipe"), lax.axis_size("dp")
    groups = lax.axis_size("tensor")
    chips = replicas // 2
    section, place, group = lax.axis_index("pipe"), lax.axis_index("dp"), lax.axis_index("tensor")
    before, after = lax.rem(section + pipe_count - 1, pipe_count), lax.rem(section + 1, pipe_count)
    right, left = lax.rem(group + 1, groups), lax.rem(group + groups - 1, groups)
    far = lax.rem(group + 2, groups)
    micro, tokens, width = cotangent.shape
    edge = codes_out.shape[-1]
    slots = errors.shape[1]
    blocks = width // edge

    def load_in(block):
        span = pl.ds(pl.multiple_of(block * edge, edge), edge)
        return pltpu.make_async_copy(
            activations.at[:, :, span], held_in.at[block], in_sem.at[block]
        )

    picked = groups * slots
    first = slots // 2

    def err_slots(origin, start=0, count=slots):
        return held_err.at[pl.ds(origin * slots + start, count)]

    barrier = pltpu.get_barrier_semaphore()
    for name, other in (
        ("tensor", right), ("tensor", left), ("pipe", before), ("pipe", after),
    ):
        pl.semaphore_signal(barrier, inc=1, device_id={name: other}, device_id_type=MESH)

    chip, core = place // 2, place % 2

    def replica(shift, which):
        return lax.rem(chip + shift + chips, chips) * 2 + which

    near = [replica(shift, which) for shift in (1, -1) for which in (0, 1)]
    for other in near + [replica(0, 1 - core)]:
        pl.semaphore_signal(barrier, inc=1, device_id={"dp": other}, device_id_type=MESH)

    list_loads = [
        pltpu.make_async_copy(source, target, list_sems.at[number])
        for number, (source, target) in enumerate(
            ((all_picks, picks), (all_picks, pick_scalars), (all_owners, owners))
        )
    ]
    for copy in list_loads:
        copy.start()
    pl.semaphore_wait(barrier, 9)

    def remote(source, target, sems, slot, device):
        return pltpu.make_async_remote_copy(
            src_ref=source, dst_ref=target,
            send_sem=sems.at[(0,) + slot], recv_sem=sems.at[(1,) + slot],
            device_id=device, device_id_type=MESH,
        )

    def columns(origin, part):
        return held_out.at[pl.ds(origin * blocks, blocks), part]

    pipe_copies = []
    for part in range(micro):
        for block in range(blocks):
            copy = remote(
                cotangent.at[part, :, pl.ds(block * edge, edge)],
                held_out.at[group * blocks + block, part],
                pipe_sems, (part, block), {"pipe": before},
            )
            copy.start()
            pipe_copies.append(copy)
    error_copies, through = [], []
    spans = (0, first), (first, slots - first)
    for way, other in enumerate((right, left)):
        start, count = spans[way]
        copy = remote(
            errors.at[far, pl.ds(start, count)], passing.at[pl.ds(start, count)],
            error_sems, (way,), {"tensor": other},
        )
        copy.start()
        through.append(copy)
    for way, other in enumerate((right, left)):
        copy = remote(
            errors.at[other], err_slots(group), error_sems, (2 + way,), {"tensor": other}
        )
        copy.start()
        error_copies.append(copy)

    @pl.loop(0, held_in.shape[0])
    def _(block):
        load_in(block).start()

    load_err = pltpu.make_async_copy(errors.at[group], err_slots(group), own_sem)
    load_err.start()

    def list_tables():
        lanes = lax.broadcasted_iota(jnp.int32, (1, replicas), 1)
        row_of = jnp.zeros((1, replicas), jnp.int32)
        owned = [place, replica(RELAY, core), replica(-RELAY, core)]
        wanted = [0 for _ in owned]
        for row in range(held_in.shape[0]):
            row_of += hit(lanes, owners[row]) * row
            wanted = [was + hit(owners[row], who) * row for was, who in zip(wanted, owned)]
        sends = jnp.zeros((1, replicas), jnp.int32)
        hears = [jnp.zeros((1, replicas), jnp.int32) for _ in owned]
        for pick in range(picked):
            at = pick // slots, pick % slots
            row = pick_scalars[at + (0, place)]
            column = pick_scalars[at + (1, place)] + at[0] * blocks
            sends += hit(row_of, row) * ((row * groups * blocks + column) * picked + pick)
            every_row = picks[at + (pl.ds(0, 1),)]
            every_column = picks[at + (pl.ds(1, 1),)] + (at[0] * blocks + 1)
            hears = [was + hit(every_row, row) * every_column for was, row in zip(hears, wanted)]
        listed[0:1, 0:replicas] = sends
        for number, columns in enumerate(hears):
            listed[number + 1 : number + 2, 0:replicas] = columns - 1

    def meet(number):
        distance = 2**number
        for way, shift in enumerate((distance, -distance)):
            for which in (0, 1):
                pl.semaphore_signal(
                    near_sems.at[number, way * 2 + core], inc=1,
                    device_id={"dp": replica(shift, which)}, device_id_type=MESH,
                )
        for slot in range(4):
            pl.semaphore_wait(near_sems.at[number, slot], 1)

    meetings = near_sems.shape[0]
    early = meetings - 1
    for copy in list_loads:
        copy.wait()
    list_tables()
    for number in range(early):
        meet(number)
    load_table = pltpu.make_async_copy(listed, table, table_sem)
    load_table.start()
    for way, (origin, other) in enumerate(((left, right), (right, left))):
        start, count = spans[way]
        through[way].wait_recv()
        copy = remote(
            passing.at[pl.ds(start, count)], err_slots(origin, start, count),
            error_sems, (4 + way,), {"tensor": other},
        )
        copy.start()
        error_copies.append(copy)

    to_right, to_left, onward = [], [], []
    for part in range(micro):
        for block in range(blocks):
            pipe_copies[part * blocks + block].wait_recv()
        own = columns(group, part)
        copy = remote(own, own, column_sems, (0, part), {"tensor": right})
        copy.start()
        to_right.append(copy)
        copy = remote(own, own, column_sems, (1, part), {"tensor": left})
        copy.start()
        to_left.append(copy)
    for number in range(early, meetings):
        meet(number)
    for part in range(micro):
        if part % 2 == 0:
            to_left[part].wait_recv()
            piece = columns(right, part)
            copy = remote(piece, piece, column_sems, (2, part), {"tensor": left})
        else:
            to_right[part].wait_recv()
            piece = columns(left, part)
            copy = remote(piece, piece, column_sems, (2, part), {"tensor": right})
        copy.start()
        onward.append(copy)

    @pl.loop(0, held_in.shape[0])
    def _(block):
        load_in(block).wait()

    load_err.wait()
    load_table.wait()
    for copy in error_copies:
        copy.wait_recv()
    for part in range(micro):
        if part % 2 == 0:
            to_right[part].wait_recv()
        else:
            to_left[part].wait_recv()
    for copy in onward:
        copy.wait_recv()

    half = chips // 2
    gathered = 2 * (half - RELAY) - 1
    relayed = 2 * gathered
    direct_in = 2 * (gathered + 1)
    strips_in = direct_in + 5
    strips_out = replicas
    width_all = groups * blocks

    def post(source, target, device):
        return [
            pltpu.make_async_remote_copy(
                src_ref=out.at[source], dst_ref=into.at[target],
                send_sem=send.at[source], recv_sem=recv.at[target],
                device_id={"dp": device}, device_id_type=MESH,
            )
            for out, into, send, recv in (
                (codes_out, codes_in, code_send, code_recv),
                (steps_out, steps_in, step_send, step_recv),
            )
        ]

    def far_tile(index):
        turn = index + 2
        distance = half - turn // 4
        across = distance == half
        flip = jnp.where(across, turn % 2, (turn // 2) % 2)
        side = jnp.where(across, core, turn % 2)
        way = 1 - 2 * side
        which = lax.rem(core + flip, 2)
        slot = jnp.where(across, 0, 1 + (half - 1 - distance) * 2 + flip)
        return (
            replica(way * distance, which), replica(way * (distance - RELAY), which),
            side * (gathered + 1) + slot,
        )

    near_tiles = []
    for side, way in enumerate((1, -1)):
        near_tiles.append((
            replica(way * RELAY, 1 - core), replica(0, 1 - core), side * (gathered + 1) + gathered
        ))
    for side, way in enumerate((1, -1)):
        near_tiles.append((replica(way * RELAY, core), None, None))
    for flip in (0, 1):
        for side, way in enumerate((1, -1)):
            which = lax.rem(core + flip, 2)
            other = replica(way, which)
            near_tiles.append((other, other, direct_in + side * 2 + flip))
    other = replica(0, 1 - core)
    near_tiles.append((other, other, direct_in + 4))
    near_tiles.append((place, None, None))
    kept = relayed + 2

    def encode(value, slot):
        reach = jnp.maximum(jnp.max(jnp.abs(value), axis=0, keepdims=True), 1e-30)
        codes = jnp.round(value * (LEVELS / reach)).astype(jnp.int32)
        codes_out[slot] = codes.astype(jnp.int16)
        steps_out[slot] = reach * (1.0 / LEVELS)

    def decode(codes, steps, slot):
        return codes[slot].astype(jnp.int32).astype(jnp.float32) * steps[slot]

    def make_tile(index, target):
        entry = table[0, target]
        pick, entry = lax.rem(entry, picked), lax.div(entry, picked)
        column, row = lax.rem(entry, width_all), lax.div(entry, width_all)
        source = held_in[row].reshape(micro * tokens, edge)
        sink = held_out[column].reshape(micro * tokens, edge)
        tile = lax.dot_general(
            source, sink, (((0,), (0,)), ((), ())), preferred_element_type=jnp.float32
        )
        encode(tile + held_err[pick].astype(jnp.float32), index)

    def send_far(index):
        _, gatherer, slot = far_tile(index)
        return post(index, slot, gatherer)

    make_tile(0, far_tile(0)[0])

    @pl.loop(1, relayed)
    def _(index):
        make_tile(index, far_tile(index)[0])
        for copy in send_far(index - 1):
            copy.start()

    waiting = send_far(relayed - 1)
    sent = []
    for number, (target, device, slot) in enumerate(near_tiles):
        make_tile(relayed + number, target)
        for copy in waiting:
            copy.start()
        waiting = post(relayed + number, slot, device) if slot is not None else []
        sent += waiting
    for copy in waiting:
        copy.start()

    columns_at = lax.broadcasted_iota(jnp.int32, (width_all, edge), 0)
    sums[...] = jnp.zeros_like(sums)

    def await_slot(slot):
        for copy in post(0, slot, place):
            copy.wait_recv()

    def add_tile(number, source, codes, steps, slot):
        mark = hit(columns_at, table[1 + number, source]).astype(jnp.float32)
        value = decode(codes, steps, slot)
        for block in range(width_all):
            sums[number, :, pl.ds(block * edge, edge)] += value * mark[block : block + 1]

    sides = (1, 0), (2, 1)
    for number, side in sides:
        add_tile(number, place, codes_out, steps_out, kept + side)
        slot = side * (gathered + 1) + gathered
        await_slot(slot)
        add_tile(number, replica(0, 1 - core), codes_in, steps_in, slot)
    for number, side in sides:
        slot = side * (gathered + 1)
        await_slot(slot)
        source = replica((2 * side - 1) * (half - RELAY), side)
        add_tile(number, source, codes_in, steps_in, slot)

    @pl.loop(0, gathered - 1)
    def _(index):
        distance = half - 1 - index // 2
        which = lax.rem(core + index % 2, 2)
        for number, side in sides:
            slot = side * (gathered + 1) + 1 + index
            await_slot(slot)
            source = replica((2 * side - 1) * (distance - RELAY), which)
            add_tile(number, source, codes_in, steps_in, slot)

    waiting = []
    for block in range(width_all):
        for number, side in sides:
            spot = side * width_all + block
            encode(sums[number, :, pl.ds(block * edge, edge)], strips_out + spot)
            for copy in waiting:
                copy.start()
            device = replica((1 - 2 * side) * RELAY, core)
            waiting = post(strips_out + spot, strips_in + spot, device)
            sent += waiting
    for copy in waiting:
        copy.start()

    def store(block):
        return pltpu.make_async_copy(
            rounded.at[block], strip.at[:, pl.ds(block * edge, edge)], out_sems.at[block]
        )

    add_tile(0, place, codes_out, steps_out, replicas - 1)
    await_slot(direct_in + 4)
    add_tile(0, replica(0, 1 - core), codes_in, steps_in, direct_in + 4)
    for flip in (0, 1):
        for side in (0, 1):
            slot = direct_in + side * 2 + flip
            await_slot(slot)
            source = replica(2 * side - 1, lax.rem(core + flip, 2))
            add_tile(0, source, codes_in, steps_in, slot)
    for block in range(width_all):
        span = pl.ds(block * edge, edge)
        value = sums[0, :, span]
        for side in (0, 1):
            slot = strips_in + side * width_all + block
            await_slot(slot)
            value = value + decode(codes_in, steps_in, slot)
        rounded[block] = value.astype(strip.dtype)
        if block > 0:
            store(block - 1).start()
    store(width_all - 1).start()

    for copy in pipe_copies + through + error_copies + to_right + to_left + onward + sent:
        copy.wait_send()

    @pl.loop(0, relayed)
    def _(index):
        for copy in send_far(index):
            copy.wait_send()

    for block in range(width_all):
        store(block).wait()


def body(activations, cotangent, error_tiles, tile_picks, row_owners):
    edge = error_tiles.shape[-1]
    groups, replicas = lax.axis_size("tensor"), lax.axis_size("dp")
    micro, tokens, features = activations.shape[1:]
    width = cotangent.shape[-1]
    slots = error_tiles.shape[4]
    picks = jnp.transpose(tile_picks[0, :, 0], (1, 2, 3, 0))
    strips = 2 * groups * width // edge
    outbox = replicas + strips
    inbox = 4 * (replicas // 4 - RELAY) + 5 + strips
    meetings = max(1, (replicas // 2 - 1).bit_length()) - 1
    hbm = pl.BlockSpec(memory_space=pl.ANY)
    dma = pltpu.SemaphoreType.DMA
    strip = pl.pallas_call(
        kernel,
        out_shape=jax.ShapeDtypeStruct((edge, groups * width), jnp.bfloat16),
        in_specs=[hbm] * 5,
        out_specs=hbm,
        scratch_shapes=[
            pltpu.VMEM(picks.shape, jnp.int32),
            pltpu.SMEM(picks.shape, jnp.int32),
            pltpu.SMEM(row_owners.shape[2:], jnp.int32),
            pltpu.VMEM((groups * width // edge, edge, edge), jnp.bfloat16),
            pltpu.VMEM((features // edge, micro, tokens, edge), jnp.bfloat16),
            pltpu.VMEM((groups * width // edge, micro, tokens, edge), jnp.bfloat16),
            pltpu.VMEM((groups * slots, edge, edge), jnp.bfloat16),
            pltpu.VMEM((slots, edge, edge), jnp.bfloat16),
            pltpu.VMEM((outbox, edge, edge), jnp.int16),
            pltpu.VMEM((outbox, 1, edge), jnp.float32),
            pltpu.VMEM((inbox, edge, edge), jnp.int16),
            pltpu.VMEM((inbox, 1, edge), jnp.float32),
            pltpu.VMEM((3, edge, groups * width), jnp.float32),
            pltpu.VMEM((4, 128), jnp.int32),
            pltpu.SMEM((4, 128), jnp.int32),
            dma((3,)), dma((groups * width // edge,)),
            dma((features // edge,)), dma(()), dma(()), dma((2, micro, width // edge)),
            dma((2, 6)), dma((2, 3, micro)),
            dma((outbox,)), dma((inbox,)), dma((outbox,)), dma((inbox,)),
            pltpu.SemaphoreType.REGULAR((max(1, meetings), 4)),
        ],
        compiler_params=pltpu.CompilerParams(
            collective_id=0, has_side_effects=True, vmem_limit_bytes=60 << 20
        ),
    )(
        picks, row_owners[0, 0],
        activations.reshape(micro, tokens, features),
        cotangent.reshape(micro, tokens, width),
        error_tiles.reshape(groups, slots, edge, edge),
    )
    return strip.reshape(1, 1, edge, groups * width)


def solution(mesh):
    in_specs = (
        P("pipe", None, "dp", "tensor"),
        P("pipe", None, "dp", "tensor"),
        P("pipe", "dp", "tensor", None, None, None, None),
        P("pipe", None, "tensor", None, None, None),
        P("pipe", "tensor", None),
    )
    out_specs = P("pipe", "tensor", "dp", None)
    return jax.shard_map(body, mesh=mesh, in_specs=in_specs, out_specs=out_specs, check_vma=False)
```

```python
import jax
import jax.numpy as jnp
from jax import lax
from jax.experimental import pallas as pl
from jax.experimental.pallas import tpu as pltpu
from jax.sharding import PartitionSpec as P

MESH = pl.DeviceIdType.MESH
LEVELS = 32767.0
RELAY = 2


def hit(left, right):
    apart = left - right
    return 1 - jnp.minimum(apart * apart, 1)


def kernel(
    all_picks, all_owners, activations, cotangent, errors, strip,
    picks, pick_scalars, owners, rounded,
    held_in, held_out, held_err, passing, codes_out, steps_out, codes_in, steps_in, sums, listed,
    table, list_sems, out_sems, in_sem, own_sem, table_sem, pipe_sems, far_sems, error_sems, column_sems,
    code_send, code_recv, step_send, step_recv, near_sems,
):
    pipe_count, replicas = lax.axis_size("pipe"), lax.axis_size("dp")
    groups = lax.axis_size("tensor")
    chips = replicas // 2
    section, place, group = lax.axis_index("pipe"), lax.axis_index("dp"), lax.axis_index("tensor")
    before, after = lax.rem(section + pipe_count - 1, pipe_count), lax.rem(section + 1, pipe_count)
    right, left = lax.rem(group + 1, groups), lax.rem(group + groups - 1, groups)
    far = lax.rem(group + 2, groups)
    micro, tokens, width = cotangent.shape
    edge = codes_out.shape[-1]
    slots = errors.shape[1]
    blocks = width // edge

    def load_in(block):
        span = pl.ds(pl.multiple_of(block * edge, edge), edge)
        return pltpu.make_async_copy(
            activations.at[:, :, span], held_in.at[block], in_sem.at[block]
        )

    picked = groups * slots
    first = slots // 2

    def err_slots(origin, start=0, count=slots):
        return held_err.at[pl.ds(origin * slots + start, count)]

    barrier = pltpu.get_barrier_semaphore()
    for name, other in (
        ("tensor", right), ("tensor", left), ("pipe", before), ("pipe", after),
    ):
        pl.semaphore_signal(barrier, inc=1, device_id={name: other}, device_id_type=MESH)
    for other in (before, after):
        pl.semaphore_signal(
            barrier, inc=1, device_id={"pipe": other, "tensor": far}, device_id_type=MESH
        )

    chip, core = place // 2, place % 2

    def replica(shift, which):
        return lax.rem(chip + shift + chips, chips) * 2 + which

    near = [replica(shift, which) for shift in (1, -1) for which in (0, 1)]
    for other in near + [replica(0, 1 - core)]:
        pl.semaphore_signal(barrier, inc=1, device_id={"dp": other}, device_id_type=MESH)

    list_loads = [
        pltpu.make_async_copy(source, target, list_sems.at[number])
        for number, (source, target) in enumerate(
            ((all_picks, picks), (all_picks, pick_scalars), (all_owners, owners))
        )
    ]
    for copy in list_loads:
        copy.start()
    pl.semaphore_wait(barrier, 11)

    def remote(source, target, sems, slot, device):
        return pltpu.make_async_remote_copy(
            src_ref=source, dst_ref=target,
            send_sem=sems.at[(0,) + slot], recv_sem=sems.at[(1,) + slot],
            device_id=device, device_id_type=MESH,
        )

    def columns(origin, part):
        return held_out.at[pl.ds(origin * blocks, blocks), part]

    pipe_copies = []
    for part in range(micro):
        for block in range(blocks):
            copy = remote(
                cotangent.at[part, :, pl.ds(block * edge, edge)],
                held_out.at[group * blocks + block, part],
                pipe_sems, (part, block), {"pipe": before},
            )
            copy.start()
            pipe_copies.append(copy)
    onward = []
    for part in range(micro):
        for block in range(blocks):
            copy = remote(
                cotangent.at[part, :, pl.ds(block * edge, edge)],
                held_out.at[group * blocks + block, part],
                far_sems, (part, block), {"pipe": before, "tensor": far},
            )
            copy.start()
            onward.append(copy)
    error_copies, through = [], []
    spans = (0, first), (first, slots - first)
    for way, other in enumerate((right, left)):
        start, count = spans[way]
        copy = remote(
            errors.at[far, pl.ds(start, count)], passing.at[pl.ds(start, count)],
            error_sems, (way,), {"tensor": other},
        )
        copy.start()
        through.append(copy)
    for way, other in enumerate((right, left)):
        copy = remote(
            errors.at[other], err_slots(group), error_sems, (2 + way,), {"tensor": other}
        )
        copy.start()
        error_copies.append(copy)

    @pl.loop(0, held_in.shape[0])
    def _(block):
        load_in(block).start()

    load_err = pltpu.make_async_copy(errors.at[group], err_slots(group), own_sem)
    load_err.start()

    def list_tables():
        lanes = lax.broadcasted_iota(jnp.int32, (1, replicas), 1)
        row_of = jnp.zeros((1, replicas), jnp.int32)
        owned = [place, replica(RELAY, core), replica(-RELAY, core)]
        wanted = [0 for _ in owned]
        for row in range(held_in.shape[0]):
            row_of += hit(lanes, owners[row]) * row
            wanted = [was + hit(owners[row], who) * row for was, who in zip(wanted, owned)]
        sends = jnp.zeros((1, replicas), jnp.int32)
        hears = [jnp.zeros((1, replicas), jnp.int32) for _ in owned]
        for pick in range(picked):
            at = pick // slots, pick % slots
            row = pick_scalars[at + (0, place)]
            column = pick_scalars[at + (1, place)] + at[0] * blocks
            sends += hit(row_of, row) * ((row * groups * blocks + column) * picked + pick)
            every_row = picks[at + (pl.ds(0, 1),)]
            every_column = picks[at + (pl.ds(1, 1),)] + (at[0] * blocks + 1)
            hears = [was + hit(every_row, row) * every_column for was, row in zip(hears, wanted)]
        listed[0:1, 0:replicas] = sends
        for number, columns in enumerate(hears):
            listed[number + 1 : number + 2, 0:replicas] = columns - 1

    def meet(number):
        distance = 2**number
        for way, shift in enumerate((distance, -distance)):
            for which in (0, 1):
                pl.semaphore_signal(
                    near_sems.at[number, way * 2 + core], inc=1,
                    device_id={"dp": replica(shift, which)}, device_id_type=MESH,
                )
        for slot in range(4):
            pl.semaphore_wait(near_sems.at[number, slot], 1)

    meetings = near_sems.shape[0]
    early = meetings - 1
    for copy in list_loads:
        copy.wait()
    list_tables()
    for number in range(early):
        meet(number)
    load_table = pltpu.make_async_copy(listed, table, table_sem)
    load_table.start()
    for way, (origin, other) in enumerate(((left, right), (right, left))):
        start, count = spans[way]
        through[way].wait_recv()
        copy = remote(
            passing.at[pl.ds(start, count)], err_slots(origin, start, count),
            error_sems, (4 + way,), {"tensor": other},
        )
        copy.start()
        error_copies.append(copy)

    to_right, to_left = [], []
    for part in range(micro):
        for block in range(blocks):
            pipe_copies[part * blocks + block].wait_recv()
        own = columns(group, part)
        copy = remote(own, own, column_sems, (0, part), {"tensor": right})
        copy.start()
        to_right.append(copy)
        copy = remote(own, own, column_sems, (1, part), {"tensor": left})
        copy.start()
        to_left.append(copy)
    for number in range(early, meetings):
        meet(number)
    @pl.loop(0, held_in.shape[0])
    def _(block):
        load_in(block).wait()

    load_err.wait()
    load_table.wait()
    for copy in error_copies:
        copy.wait_recv()
    for copy in to_right + to_left + onward:
        copy.wait_recv()

    half = chips // 2
    gathered = 2 * (half - RELAY) - 1
    relayed = 2 * gathered
    direct_in = 2 * (gathered + 1)
    strips_in = direct_in + 5
    strips_out = replicas
    width_all = groups * blocks

    def post(source, target, device):
        return [
            pltpu.make_async_remote_copy(
                src_ref=out.at[source], dst_ref=into.at[target],
                send_sem=send.at[source], recv_sem=recv.at[target],
                device_id={"dp": device}, device_id_type=MESH,
            )
            for out, into, send, recv in (
                (codes_out, codes_in, code_send, code_recv),
                (steps_out, steps_in, step_send, step_recv),
            )
        ]

    def far_tile(index):
        turn = index + 2
        distance = half - turn // 4
        across = distance == half
        flip = jnp.where(across, turn % 2, (turn // 2) % 2)
        side = jnp.where(across, core, turn % 2)
        way = 1 - 2 * side
        which = lax.rem(core + flip, 2)
        slot = jnp.where(across, 0, 1 + (half - 1 - distance) * 2 + flip)
        return (
            replica(way * distance, which), replica(way * (distance - RELAY), which),
            side * (gathered + 1) + slot,
        )

    near_tiles = []
    for side, way in enumerate((1, -1)):
        near_tiles.append((
            replica(way * RELAY, 1 - core), replica(0, 1 - core), side * (gathered + 1) + gathered
        ))
    for side, way in enumerate((1, -1)):
        near_tiles.append((replica(way * RELAY, core), None, None))
    for flip in (0, 1):
        for side, way in enumerate((1, -1)):
            which = lax.rem(core + flip, 2)
            other = replica(way, which)
            near_tiles.append((other, other, direct_in + side * 2 + flip))
    other = replica(0, 1 - core)
    near_tiles.append((other, other, direct_in + 4))
    near_tiles.append((place, None, None))
    kept = relayed + 2

    def encode(value, slot):
        reach = jnp.maximum(jnp.max(jnp.abs(value), axis=0, keepdims=True), 1e-30)
        codes = jnp.round(value * (LEVELS / reach)).astype(jnp.int32)
        codes_out[slot] = codes.astype(jnp.int16)
        steps_out[slot] = reach * (1.0 / LEVELS)

    def decode(codes, steps, slot):
        return codes[slot].astype(jnp.int32).astype(jnp.float32) * steps[slot]

    def make_tile(index, target):
        entry = table[0, target]
        pick, entry = lax.rem(entry, picked), lax.div(entry, picked)
        column, row = lax.rem(entry, width_all), lax.div(entry, width_all)
        source = held_in[row].reshape(micro * tokens, edge)
        sink = held_out[column].reshape(micro * tokens, edge)
        tile = lax.dot_general(
            source, sink, (((0,), (0,)), ((), ())), preferred_element_type=jnp.float32
        )
        encode(tile + held_err[pick].astype(jnp.float32), index)

    def send_far(index):
        _, gatherer, slot = far_tile(index)
        return post(index, slot, gatherer)

    make_tile(0, far_tile(0)[0])

    @pl.loop(1, relayed)
    def _(index):
        make_tile(index, far_tile(index)[0])
        for copy in send_far(index - 1):
            copy.start()

    waiting = send_far(relayed - 1)
    sent = []
    for number, (target, device, slot) in enumerate(near_tiles):
        make_tile(relayed + number, target)
        for copy in waiting:
            copy.start()
        waiting = post(relayed + number, slot, device) if slot is not None else []
        sent += waiting
    for copy in waiting:
        copy.start()

    columns_at = lax.broadcasted_iota(jnp.int32, (width_all, edge), 0)
    sums[...] = jnp.zeros_like(sums)

    def await_slot(slot):
        for copy in post(0, slot, place):
            copy.wait_recv()

    def add_tile(number, source, codes, steps, slot):
        mark = hit(columns_at, table[1 + number, source]).astype(jnp.float32)
        value = decode(codes, steps, slot)
        for block in range(width_all):
            sums[number, :, pl.ds(block * edge, edge)] += value * mark[block : block + 1]

    sides = (1, 0), (2, 1)
    for number, side in sides:
        add_tile(number, place, codes_out, steps_out, kept + side)
        slot = side * (gathered + 1) + gathered
        await_slot(slot)
        add_tile(number, replica(0, 1 - core), codes_in, steps_in, slot)
    for number, side in sides:
        slot = side * (gathered + 1)
        await_slot(slot)
        source = replica((2 * side - 1) * (half - RELAY), side)
        add_tile(number, source, codes_in, steps_in, slot)

    @pl.loop(0, gathered - 1)
    def _(index):
        distance = half - 1 - index // 2
        which = lax.rem(core + index % 2, 2)
        for number, side in sides:
            slot = side * (gathered + 1) + 1 + index
            await_slot(slot)
            source = replica((2 * side - 1) * (distance - RELAY), which)
            add_tile(number, source, codes_in, steps_in, slot)

    waiting = []
    for block in range(width_all):
        for number, side in sides:
            spot = side * width_all + block
            encode(sums[number, :, pl.ds(block * edge, edge)], strips_out + spot)
            for copy in waiting:
                copy.start()
            device = replica((1 - 2 * side) * RELAY, core)
            waiting = post(strips_out + spot, strips_in + spot, device)
            sent += waiting
    for copy in waiting:
        copy.start()

    def store(block):
        return pltpu.make_async_copy(
            rounded.at[block], strip.at[:, pl.ds(block * edge, edge)], out_sems.at[block]
        )

    add_tile(0, place, codes_out, steps_out, replicas - 1)
    await_slot(direct_in + 4)
    add_tile(0, replica(0, 1 - core), codes_in, steps_in, direct_in + 4)
    for flip in (0, 1):
        for side in (0, 1):
            slot = direct_in + side * 2 + flip
            await_slot(slot)
            source = replica(2 * side - 1, lax.rem(core + flip, 2))
            add_tile(0, source, codes_in, steps_in, slot)
    for block in range(width_all):
        span = pl.ds(block * edge, edge)
        value = sums[0, :, span]
        for side in (0, 1):
            slot = strips_in + side * width_all + block
            await_slot(slot)
            value = value + decode(codes_in, steps_in, slot)
        rounded[block] = value.astype(strip.dtype)
        if block > 0:
            store(block - 1).start()
    store(width_all - 1).start()

    for copy in pipe_copies + through + error_copies + to_right + to_left + onward + sent:
        copy.wait_send()

    @pl.loop(0, relayed)
    def _(index):
        for copy in send_far(index):
            copy.wait_send()

    for block in range(width_all):
        store(block).wait()


def body(activations, cotangent, error_tiles, tile_picks, row_owners):
    edge = error_tiles.shape[-1]
    groups, replicas = lax.axis_size("tensor"), lax.axis_size("dp")
    micro, tokens, features = activations.shape[1:]
    width = cotangent.shape[-1]
    slots = error_tiles.shape[4]
    picks = jnp.transpose(tile_picks[0, :, 0], (1, 2, 3, 0))
    strips = 2 * groups * width // edge
    outbox = replicas + strips
    inbox = 4 * (replicas // 4 - RELAY) + 5 + strips
    meetings = max(1, (replicas // 2 - 1).bit_length()) - 1
    hbm = pl.BlockSpec(memory_space=pl.ANY)
    dma = pltpu.SemaphoreType.DMA
    strip = pl.pallas_call(
        kernel,
        out_shape=jax.ShapeDtypeStruct((edge, groups * width), jnp.bfloat16),
        in_specs=[hbm] * 5,
        out_specs=hbm,
        scratch_shapes=[
            pltpu.VMEM(picks.shape, jnp.int32),
            pltpu.SMEM(picks.shape, jnp.int32),
            pltpu.SMEM(row_owners.shape[2:], jnp.int32),
            pltpu.VMEM((groups * width // edge, edge, edge), jnp.bfloat16),
            pltpu.VMEM((features // edge, micro, tokens, edge), jnp.bfloat16),
            pltpu.VMEM((groups * width // edge, micro, tokens, edge), jnp.bfloat16),
            pltpu.VMEM((groups * slots, edge, edge), jnp.bfloat16),
            pltpu.VMEM((slots, edge, edge), jnp.bfloat16),
            pltpu.VMEM((outbox, edge, edge), jnp.int16),
            pltpu.VMEM((outbox, 1, edge), jnp.float32),
            pltpu.VMEM((inbox, edge, edge), jnp.int16),
            pltpu.VMEM((inbox, 1, edge), jnp.float32),
            pltpu.VMEM((3, edge, groups * width), jnp.float32),
            pltpu.VMEM((4, 128), jnp.int32),
            pltpu.SMEM((4, 128), jnp.int32),
            dma((3,)), dma((groups * width // edge,)),
            dma((features // edge,)), dma(()), dma(()), dma((2, micro, width // edge)), dma((2, micro, width // edge)),
            dma((2, 6)), dma((2, 2, micro)),
            dma((outbox,)), dma((inbox,)), dma((outbox,)), dma((inbox,)),
            pltpu.SemaphoreType.REGULAR((max(1, meetings), 4)),
        ],
        compiler_params=pltpu.CompilerParams(
            collective_id=0, has_side_effects=True, vmem_limit_bytes=60 << 20
        ),
    )(
        picks, row_owners[0, 0],
        activations.reshape(micro, tokens, features),
        cotangent.reshape(micro, tokens, width),
        error_tiles.reshape(groups, slots, edge, edge),
    )
    return strip.reshape(1, 1, edge, groups * width)


def solution(mesh):
    in_specs = (
        P("pipe", None, "dp", "tensor"),
        P("pipe", None, "dp", "tensor"),
        P("pipe", "dp", "tensor", None, None, None, None),
        P("pipe", None, "tensor", None, None, None),
        P("pipe", "tensor", None),
    )
    out_specs = P("pipe", "tensor", "dp", None)
    return jax.shard_map(body, mesh=mesh, in_specs=in_specs, out_specs=out_specs, check_vma=False)
```
